256 devices in a mesh: section: 8 (over z), lon: 32 (over y, x, core).
Axes of the slice: x: 4, y: 4, z: 8, core: 2. Of those that a mesh axis runs over, the one named last changes fastest.
Arguments:
- lanczos_block: bfloat16 [16, 8, 256, 512], P(None, None, 'lon'), may hold values from -9 to 9
- previous: bfloat16 [16, 8, 256, 512], P(None, 'section', 'lon'), may hold values from -6 to 6
- beta_prev: float32 [16, 16], replicated, may hold values from -2 to 2, as said below
- weights: bfloat16 [8, 9, 512, 512], P('section'), may hold values from -0.09375 to 0.09375
- act_slope: bfloat16 [8, 8, 256, 512], P('section', None, 'lon'), may hold values from 0 to 1.09375
- metric: float32 [8, 256], P(None, 'lon'), may hold values from 0.3 to 3
Outputs:
- residual_block: float32 [16, 8, 256, 512], P(None, 'section', 'lon')
- projection: float32 [16, 16], replicated
- residual_gram: float32 [16, 16], replicated
The draws below stay inside these ranges and needn't reach their ends.
Inputs may be any that keep to these rules, and one draw needn't show every extreme that they name: `beta_prev`: upper triangular, with a positive diagonal.
All inputs are finite; a program needn't handle non-finite values.
Results may differ from the reference program's by a relative error of at most 0.02.
Values may be sent and summed in bfloat16 or wider, within the bound.
No kernel may reach another device: no remote copies, remote signals or barrier semaphores. Data moves between devices by JAX's collectives and lax.ppermute only.
A program may use at most 64 MiB of HBM per device.

```python
import math
import jax
import jax.numpy as jnp
from jax import lax

C = 512
K = 16
DILATION_SIZE = 4
LAT = 8
LON = 256
LAYERS = 8


def draw_lanczos_block(key, part):
    lat_pos = jnp.arange(LAT, dtype=jnp.float32) / max(LAT - 1, 1)
    lon_pos = jnp.arange(LON, dtype=jnp.float32) / max(LON - 1, 1)
    amplitude = 0.5 * jnp.sqrt((1.0 + 2.0 * lat_pos)[:, None] * (1.0 + 2.0 * lon_pos)[None, :])
    base_values = jax.random.normal(key, (K, LAT, LON, C), jnp.float32)
    base_values = jnp.clip(base_values, -6.0, 6.0)
    return (base_values * amplitude[None, :, :, None]).astype(jnp.bfloat16)


def draw_beta_prev(key, part):
    first_key, second_key = jax.random.split(key)
    diagonal_part = jax.random.uniform(first_key, (K,), jnp.float32, 0.5, 1.5)
    upper_part = jnp.clip(0.3 * jax.random.normal(second_key, (K, K), jnp.float32), -1.5, 1.5)
    return jnp.triu(upper_part, 1) + jnp.diag(diagonal_part)


def steps_of(stream_key, shape, shards, least, largest):
    def one(axis_at, shards_of):
        draws = jax.random.uniform(jax.random.fold_in(jax.random.fold_in(stream_key, 6), axis_at), (shards_of,), jnp.float32, least / len(shards), largest / len(shards))
        return jnp.repeat(jnp.exp(draws), shape[axis_at] // shards_of).reshape((-1,) + (1,) * (len(shape) - axis_at - 1))

    loudness = one(*shards[0])
    for cut in shards[1:]:
        loudness = loudness * one(*cut)
    return loudness


def gaussian(rng, dims, spread, bound, cuts=(), held_as=jnp.bfloat16):
    array = spread * jax.random.normal(rng, dims, jnp.float32)
    if cuts:
        array = array * steps_of(rng, dims, cuts, -0.22, 0.18)
    return jnp.clip(array, -bound, bound).astype(held_as)


def setup_inputs(seed: int = 0) -> dict:
    keys = jax.random.split(jax.random.key(seed), 7)
    return {
        "lanczos_block": draw_lanczos_block(jax.random.fold_in(keys[6], 71), 0),
        "previous": gaussian(keys[1], (K, LAT, LON, C), 1.0, 6.0, ((1, 8), (2, 32))),
        "beta_prev": draw_beta_prev(jax.random.fold_in(keys[6], 71), 0),
        "weights": gaussian(keys[3], (LAYERS, 9, C, C), (9 * C) ** -0.5, 0.09375, ((0, 8),)),
        "act_slope": jnp.clip(1.09375 * jax.random.uniform(keys[4], (LAYERS, LAT, LON, C), jnp.float32) ** steps_of(keys[4], (LAYERS, LAT, LON, C), ((0, 8), (2, 32)), -0.2, 0.2), 0.0, 1.09375).astype(jnp.bfloat16),
        "metric": jnp.clip(jnp.exp(math.log(3.0) - 2.3025851 * jax.random.uniform(keys[5], (LAT, LON), jnp.float32) ** steps_of(keys[5], (LAT, LON), ((1, 32),), -0.2, 0.2)), 0.3, 3.0),
    }


def shifted_tap(input_field, row_stride, column_stride, direction_sign):
    rolled_field = jnp.roll(input_field, -direction_sign * column_stride * DILATION_SIZE, axis=2)
    padded_field = jnp.pad(rolled_field, ((0, 0), (DILATION_SIZE, DILATION_SIZE), (0, 0), (0, 0)))
    first_row = DILATION_SIZE + direction_sign * row_stride * DILATION_SIZE
    return padded_field[:, first_row:first_row + LAT]


def convolve(input_field, tap_weights, direction_sign):
    summed = jnp.zeros((input_field.shape[0] * LAT * LON, C), jnp.float32)
    for row_stride in (-1, 0, 1):
        for column_stride in (-1, 0, 1):
            tap_index = 3 * (row_stride + 1) + (column_stride + 1)
            tap_rows = shifted_tap(input_field, row_stride, column_stride, direction_sign).reshape(-1, C)
            tap_matrix = tap_weights[tap_index]
            if direction_sign < 0:
                tap_matrix = tap_matrix.T
            summed = summed + jnp.dot(tap_rows, tap_matrix, preferred_element_type=jnp.float32)
    return summed.reshape(input_field.shape)


def reference(lanczos_block, previous, beta_prev, weights, act_slope, metric):
    tangent = lanczos_block
    for layer_index in range(LAYERS):
        convolved = convolve(tangent, weights[layer_index], 1)
        slope_now = act_slope[layer_index].astype(jnp.float32)[None]
        tangent = (tangent.astype(jnp.float32) + slope_now * convolved).astype(jnp.bfloat16)
    cotangent = (metric[None, :, :, None] * tangent.astype(jnp.float32)).astype(jnp.bfloat16)
    for layer_index in range(LAYERS - 1, -1, -1):
        slope_now = act_slope[layer_index].astype(jnp.float32)[None]
        sensitivity = (slope_now * cotangent.astype(jnp.float32)).astype(jnp.bfloat16)
        convolved = convolve(sensitivity, weights[layer_index], -1)
        cotangent = (cotangent.astype(jnp.float32) + convolved).astype(jnp.bfloat16)
    cell_count = LAT * LON * C
    high = lax.Precision.HIGHEST
    block_flat = lanczos_block.reshape(K, -1).astype(jnp.float32)
    prev_flat = previous.reshape(K, -1).astype(jnp.float32)
    shifted = cotangent.reshape(K, -1).astype(jnp.float32) - jnp.dot(beta_prev, prev_flat, precision=high)
    projection = jnp.dot(block_flat, shifted.T, precision=high) / cell_count
    residual_rows = shifted - jnp.dot(projection.T, block_flat, precision=high)
    residual_gram = jnp.dot(residual_rows, residual_rows.T, precision=high) / cell_count
    return residual_rows.reshape(lanczos_block.shape), projection, residual_gram
```

```python
import jax
import jax.numpy as jnp
from jax import lax
from jax.experimental import pallas as pl
from jax.experimental.pallas import tpu as pltpu
from jax.sharding import PartitionSpec as P

K = 16
C = 512
LAYERS = 8
ROWS = 128
TAP_ROWS = 3 * C
BF = jnp.bfloat16
F32 = jnp.float32


def lon_pairs(dy, dx, dc):
    pairs = []
    for y in range(4):
        for x in range(4):
            for c in range(2):
                there = ((y + dy) % 4) * 8 + ((x + dx) % 4) * 2 + (c + dc) % 2
                pairs.append((y * 8 + x * 2 + c, there))
    return pairs


def shift_x(v, d):
    return lax.ppermute(v, "lon", lon_pairs(0, d, 0))


def shift_y(v, d):
    return lax.ppermute(v, "lon", lon_pairs(d, 0, 0))


def shift_c(v, d):
    return lax.ppermute(v, "lon", lon_pairs(0, 0, d))


def shift_z(v, d):
    return lax.ppermute(v, "section", [(i, (i + d) % 8) for i in range(8)])


def ahead(v, at):
    n = v.shape[0]
    return lax.dynamic_slice_in_dim(jnp.concatenate([v, v]), at, n, 0)


def place(parts, at):
    n = len(parts)
    v = jnp.stack(parts)
    return lax.dynamic_slice_in_dim(jnp.concatenate([v, v]), (n - at) % n, n, 0)


def swap(v, at, shift):
    n = v.shape[0]
    out = ahead(v, at)
    got = [out[0]] + [shift(out[d], d) for d in range(1, n)]
    return place([got[(n - e) % n] for e in range(n)], at)


def gather(v, at, shift, n):
    got = [v] + [shift(v, d) for d in range(1, n)]
    return place([got[(n - e) % n] for e in range(n)], at)


def rolled(half, by):
    if by == 0:
        return half
    return pltpu.roll(half, by % half.shape[0], 0)


def passes(w_hbm, x_ref, slope_ref, metric_ref, out_ref, w, cat, field, sems):
    def fetch(l):
        return pltpu.make_async_copy(w_hbm.at[l], w.at[l], sems.at[l])

    def start(l, carry):
        fetch(l).start()
        return carry

    lax.fori_loop(0, LAYERS, start, 0)
    field[...] = x_ref[...].astype(F32)

    def fill(value, sign):
        for half in range(2):
            part = value[half * 64 : half * 64 + 64]
            for b in range(3):
                cat[half * 64 : half * 64 + 64, b * C : (b + 1) * C] = rolled(
                    part, -sign * (b - 1)
                ).astype(BF)

    def forward(l, carry):
        fetch(l).wait()
        now = field[...]
        fill(now, 1)
        mid = jnp.dot(cat[...], w[l, TAP_ROWS : 2 * TAP_ROWS], preferred_element_type=F32)
        up = jnp.dot(cat[64:], w[l, 2 * TAP_ROWS :], preferred_element_type=F32)
        down = jnp.dot(cat[:64], w[l, :TAP_ROWS], preferred_element_type=F32)
        slope = slope_ref[l].astype(F32)
        conv = mid + jnp.concatenate([up, down], 0)
        field[...] = (now + slope * conv).astype(BF).astype(F32)
        return carry

    lax.fori_loop(0, LAYERS, forward, 0)
    parts = metric_ref[...].astype(F32)
    scale = parts[:, :128] + parts[:, 128:256] + parts[:, 256:384]
    scale = jnp.concatenate([scale] * 4, 1)
    field[...] = (scale * field[...]).astype(BF).astype(F32)

    def backward(i, carry):
        l = LAYERS - 1 - i
        now = field[...]
        sens = (slope_ref[l].astype(F32) * now).astype(BF).astype(F32)
        fill(sens, -1)
        mid = jnp.zeros((ROWS, C), F32)
        up = jnp.zeros((ROWS // 2, C), F32)
        down = jnp.zeros((ROWS // 2, C), F32)
        dims = (((1,), (1,)), ((), ()))
        for b in range(3):
            cols = slice(b * C, (b + 1) * C)

            def tap(a):
                return w[l, a * TAP_ROWS + b * C : a * TAP_ROWS + (b + 1) * C]

            mid += lax.dot_general(cat[:, cols], tap(1), dims, preferred_element_type=F32)
            up += lax.dot_general(cat[64:, cols], tap(0), dims, preferred_element_type=F32)
            down += lax.dot_general(cat[:64, cols], tap(2), dims, preferred_element_type=F32)
        conv = mid + jnp.concatenate([up, down], 0)
        field[...] = (now + conv).astype(BF).astype(F32)
        return carry

    lax.fori_loop(0, LAYERS, backward, 0)
    out_ref[...] = field[...].astype(BF)


def run_passes(w_all, unit, slopes, metric):
    vmem = pl.BlockSpec(memory_space=pltpu.VMEM)
    return pl.pallas_call(
        passes,
        out_shape=jax.ShapeDtypeStruct((ROWS, C), BF),
        in_specs=[pl.BlockSpec(memory_space=pl.ANY), vmem, vmem, vmem],
        out_specs=vmem,
        scratch_shapes=[
            pltpu.VMEM((LAYERS, 9 * C, C), BF),
            pltpu.VMEM((ROWS, TAP_ROWS), BF),
            pltpu.VMEM((ROWS, C), F32),
            pltpu.SemaphoreType.DMA((LAYERS,)),
        ],
        compiler_params=pltpu.CompilerParams(vmem_limit_bytes=60 * 1024 * 1024),
    )(w_all, unit, slopes, metric)


def to_units(lanczos_block, act_slope, metric, z, y, x, c):
    r, h = z % 4, z // 4
    block = lax.dynamic_slice_in_dim(lanczos_block, h * 8, 8, 0)
    block = block.reshape(8, 2, 4, 8, C)
    block = lax.dynamic_index_in_dim(block, r, 2, keepdims=False)
    slope = act_slope[0].reshape(2, 4, 8, C).transpose(1, 0, 2, 3)
    slope = jnp.concatenate([slope, slope])
    slope = swap(slope, z, shift_z)
    head = lax.reduce_precision(metric, 8, 7)
    rest = metric - head
    middle = lax.reduce_precision(rest, 8, 7)
    low = rest - middle
    parts = jnp.stack([head, middle, low, jnp.zeros_like(low)], -1).astype(BF)
    parts = lax.dynamic_index_in_dim(parts.reshape(2, 4, 8, 4), r, 1, keepdims=False)
    parts = jnp.broadcast_to(parts[..., None], (2, 8, 4, 128)).reshape(1, 2, 8, C)
    both = jnp.concatenate([block, slope, parts])
    both = both.reshape(17, 2, 2, 4, C).transpose(3, 0, 1, 2, 4)
    both = swap(both, x, shift_x)
    block = both[:, :8].reshape(4, 4, 2, 2, 2, C).transpose(1, 2, 0, 3, 4, 5)
    fixed = jnp.broadcast_to(both[None, :, 8:], (4, 4, 9, 2, 2, C))
    fixed = fixed.transpose(0, 2, 1, 3, 4, 5)
    both = jnp.concatenate([block, fixed], 1)
    both = swap(both, y, shift_y)
    mine = lax.dynamic_index_in_dim(both, c, 1, keepdims=False)
    theirs = lax.dynamic_index_in_dim(both, 1 - c, 1, keepdims=False)
    fixed = both[:, 2:]
    kept = jnp.concatenate([mine[:, None], fixed], 1)
    sent = jnp.concatenate([theirs[:, None], fixed], 1)
    both = place([kept, shift_c(sent, 1)], c)
    both = both.transpose(2, 4, 1, 3, 0, 5, 6).reshape(10, ROWS, C)
    return both[0], both[1:9], both[9]


def to_rows(unit, z, y, x, c):
    h = z // 4
    unit = unit.reshape(2, 4, 4, 2, 2, C)
    mine = lax.dynamic_index_in_dim(unit, h, 0, keepdims=False)
    theirs = lax.dynamic_index_in_dim(unit, 1 - h, 0, keepdims=False)
    both = place([mine, shift_z(theirs, 4)], h)
    both = swap(both.transpose(3, 0, 1, 2, 4, 5), c, shift_c)
    both = swap(both.transpose(3, 0, 1, 2, 4, 5), x, shift_x)
    both = swap(both.transpose(3, 0, 1, 2, 4, 5), y, shift_y)
    return both.transpose(3, 0, 2, 4, 1, 5).reshape(K, 8, C)


def all_sum(v, z, y, x, c):
    v = jnp.sum(gather(v, c, shift_c, 2), 0)
    v = jnp.sum(gather(v, x, shift_x, 4), 0)
    v = jnp.sum(gather(v, y, shift_y, 4), 0)
    v = v + shift_z(v, 4)
    return jnp.sum(gather(v, z % 4, shift_z, 4), 0)


def body(lanczos_block, previous, beta_prev, weights, act_slope, metric):
    z = lax.axis_index("section")
    b = lax.axis_index("lon")
    y, x, c = b // 8, (b // 2) % 4, b % 2
    part = lax.dynamic_slice_in_dim(weights[0].reshape(9 * C, C), b * 144, 144, 0)
    w_all = lax.all_gather(part, ("section", "lon"), tiled=True)
    unit, slopes, scale = to_units(lanczos_block, act_slope, metric, z, y, x, c)
    applied = run_passes(w_all.reshape(LAYERS, 9 * C, C), unit, slopes, scale)
    applied = to_rows(applied, z, y, x, c)
    high = lax.Precision.HIGHEST
    cells = float(8 * 256 * C)
    own = lax.dynamic_slice_in_dim(lanczos_block, z, 1, 1).reshape(K, -1).astype(F32)
    before = previous.reshape(K, -1).astype(F32)
    shifted = applied.reshape(K, -1).astype(F32) - jnp.dot(beta_prev, before, precision=high)

    def inner(u, v):
        return lax.dot_general(u, v, (((1,), (1,)), ((), ())), precision=high)

    sums = jnp.concatenate([inner(own, shifted), inner(shifted, shifted), inner(own, own)])
    sums = all_sum(sums, z, y, x, c) / cells
    projection, squares, base = sums[:K], sums[K : 2 * K], sums[2 * K :]
    residual = shifted - jnp.dot(projection.T, own, precision=high)
    cross = jnp.dot(projection.T, projection, precision=high)
    twice = jnp.dot(jnp.dot(projection.T, base, precision=high), projection, precision=high)
    gram = squares - cross - cross.T + twice
    return residual.reshape(K, 1, 8, C), projection, gram


def solution(mesh):
    return jax.shard_map(
        body,
        mesh=mesh,
        in_specs=(
            P(None, None, "lon", None),
            P(None, "section", "lon", None),
            P(),
            P("section", None, None, None),
            P("section", None, "lon", None),
            P(None, "lon"),
        ),
        out_specs=(P(None, "section", "lon", None), P(), P()),
        check_vma=False,
    )
```

```python
import functools

import jax
import jax.numpy as jnp
from jax import lax
from jax.experimental import pallas as pl
from jax.experimental.pallas import tpu as pltpu
from jax.sharding import PartitionSpec as P

K = 16
C = 512
STAGE = 4
ROWS = 128
TAP_ROWS = 3 * C
BF = jnp.bfloat16
F32 = jnp.float32


def lon_pairs(dy, dx, dc):
    pairs = []
    for y in range(4):
        for x in range(4):
            for c in range(2):
                there = ((y + dy) % 4) * 8 + ((x + dx) % 4) * 2 + (c + dc) % 2
                pairs.append((y * 8 + x * 2 + c, there))
    return pairs


def shift_x(v, d):
    return lax.ppermute(v, "lon", lon_pairs(0, d, 0))


def shift_y(v, d):
    return lax.ppermute(v, "lon", lon_pairs(d, 0, 0))


def shift_c(v, d):
    return lax.ppermute(v, "lon", lon_pairs(0, 0, d))


def ahead(v, at):
    n = v.shape[0]
    return lax.dynamic_slice_in_dim(jnp.concatenate([v, v]), at, n, 0)


def place(parts, at):
    n = len(parts)
    v = jnp.stack(parts)
    return lax.dynamic_slice_in_dim(jnp.concatenate([v, v]), (n - at) % n, n, 0)


def swap(v, at, shift):
    n = v.shape[0]
    out = ahead(v, at)
    got = [out[0]]
    for d in range(1, n):
        got.append(shift(out[d], d))
    return place([got[(n - e) % n] for e in range(n)], at)


def core_pairs(first, d):
    pairs = []
    for y in range(4):
        for x in range(4):
            for c in range(2):
                dy, dx = (0, d) if (c == 0) == first else (d, 0)
                there = ((y + dy) % 4) * 8 + ((x + dx) % 4) * 2 + c
                pairs.append((y * 8 + x * 2 + c, there))
    return pairs


def along(v, first, d):
    return lax.ppermute(v, "lon", core_pairs(first, d))


def from_layer(v, i):
    pairs = [(4 * (t % 2) + (t // 2 + i) % 4, t) for t in range(8)]
    return lax.ppermute(v, "section", pairs)


def fetch_layers(w, slope, z, y, x, c):
    f, g = jnp.where(c == 0, x, y), jnp.where(c == 0, y, x)
    own = lax.dynamic_slice_in_dim(w, c * 256 + (g * 4 + f) * 16, 16, 1).reshape(144, C)
    slope = slope.reshape(2, 4, 8, C)
    slices, slopes = [], []
    for i in range(4):
        rows = lax.dynamic_index_in_dim(slope, (z + 4 - i) % 4, 1, keepdims=False)
        got = from_layer(jnp.concatenate([own, rows.reshape(16, C)]), i)
        slices.append(got[:144].reshape(9, 16, C))
        slopes.append(got[144:].reshape(2, 8, C))
    v = jnp.stack(slices)[None]
    up = along(v, True, -1)
    down = along(v, True, 1)
    across = along(up, True, -1)
    mine = []
    for group, way in ((0, 1), (1, -1)):
        layers = slice(2 * group, 2 * group + 2)
        four = jnp.concatenate([v[:, layers], up[:, layers], across[:, layers], down[:, layers]])
        after = along(four, False, -1)
        before = along(four, False, 1)
        far = along(before if way > 0 else after, False, way)
        mine += [four, after, before, far]
    theirs = []
    for v in mine:
        theirs.append(shift_c(v, 1))
    return mine + theirs, place(slopes, z // 2)


AWAY = (0, 1, 3, 2)


def place_layer(layer, at, pieces, w, sem):
    z, y, x, c = at[0], at[1], at[2], at[3]
    i = lax.rem(layer - z // 2 + 4, 4)
    for side in range(2):
        core = c if side == 0 else 1 - c
        f, g = jnp.where(core == 0, x, y), jnp.where(core == 0, y, x)
        for group in range(2):

            @pl.when(i // 2 == group)
            def _(side=side, group=group, core=core, f=f, g=g):
                first = side * 8 + group * 4
                for part, away in zip(pieces[first : first + 4], AWAY):
                    base = core * 256 + lax.rem(g + away, 4) * 64

                    def one(e, carry, part=part, base=base):
                        spot = pl.multiple_of(base + lax.rem(f + e, 4) * 16, 16)
                        pltpu.make_async_copy(
                            part.at[e, lax.rem(i, 2)],
                            w.at[layer, :, pl.ds(spot, 16)],
                            sem.at[layer],
                        ).start()
                        return carry

                    lax.fori_loop(0, 4, one, 0)


def rolled(quarter, by):
    if by == 0:
        return quarter
    return pltpu.roll(quarter, by % quarter.shape[0], 0)


def passes(stage, ahead, back, at, x_ref, slope_ref, metric_ref, *rest):
    *pieces, out_ref, w, cat, field, sems = rest
    active = lax.rem(at[0], 2) == stage

    @pl.when(jnp.logical_not(active))
    def _():
        out_ref[...] = x_ref[...]

    def fill(value, sign):
        for quarter in range(4):
            rows = slice(quarter * 64, quarter * 64 + 64)
            for b in range(3):
                cat[rows, b * C : (b + 1) * C] = rolled(value[rows], -sign * (b - 1)).astype(BF)

    def wide(v):
        v = v.astype(F32)
        return jnp.concatenate([v[:64], v[:64], v[64:], v[64:]], 0)

    def ready(l):
        pltpu.make_async_copy(w.at[l], w.at[l], sems.at[l]).wait()

    def forward(l, carry):
        ready(l)
        now = field[...]
        fill(now, 1)

        def three(rows, a):
            taps = w[l, 3 * a : 3 * a + 3].reshape(TAP_ROWS, C)
            return jnp.dot(rows, taps, preferred_element_type=F32)

        mid, up, down = three(cat[...], 1), three(cat[128:], 2), three(cat[:128], 0)
        conv = mid + jnp.concatenate([up, down], 0)
        field[...] = (now + wide(slope_ref[l]) * conv).astype(BF).astype(F32)
        return carry

    def backward(i, carry):
        l = STAGE - 1 - i
        if not ahead:
            ready(l)
        now = field[...]
        sens = (wide(slope_ref[l]) * now).astype(BF).astype(F32)
        fill(sens, -1)
        mid = jnp.zeros((2 * ROWS, C), F32)
        up = jnp.zeros((ROWS, C), F32)
        down = jnp.zeros((ROWS, C), F32)
        dims = (((1,), (1,)), ((), ()))
        for b in range(3):
            cols = slice(b * C, (b + 1) * C)
            mid += lax.dot_general(cat[:, cols], w[l, 3 + b], dims, preferred_element_type=F32)
            up += lax.dot_general(cat[128:, cols], w[l, b], dims, preferred_element_type=F32)
            down += lax.dot_general(cat[:128, cols], w[l, 6 + b], dims, preferred_element_type=F32)
        conv = mid + jnp.concatenate([up, down], 0)
        field[...] = (now + conv).astype(BF).astype(F32)
        return carry

    @pl.when(active)
    def _():
        def issue(i, carry):
            place_layer(i if ahead else STAGE - 1 - i, at, pieces, w, sems)
            return carry

        lax.fori_loop(0, STAGE, issue, 0)
        field[...] = x_ref[...].astype(F32)
        if ahead:
            lax.fori_loop(0, STAGE, forward, 0)
        if ahead and back:
            parts = metric_ref[...].astype(F32)
            scale = parts[:, :128] + parts[:, 128:256] + parts[:, 256:384]
            scale = wide(jnp.concatenate([scale] * 4, 1))
            field[...] = (scale * field[...]).astype(BF).astype(F32)
        if back:
            lax.fori_loop(0, STAGE, backward, 0)
        out_ref[...] = field[...].astype(BF)


def run_passes(stage, ahead, back, at, unit, slopes, metric, pieces):
    vmem = pl.BlockSpec(memory_space=pltpu.VMEM)
    anywhere = pl.BlockSpec(memory_space=pl.ANY)
    return pl.pallas_call(
        functools.partial(passes, stage, ahead, back),
        out_shape=jax.ShapeDtypeStruct((2 * ROWS, C), BF),
        in_specs=[pl.BlockSpec(memory_space=pltpu.SMEM), vmem, vmem, vmem]
        + [anywhere] * len(pieces),
        out_specs=vmem,
        scratch_shapes=[
            pltpu.VMEM((STAGE, 9, C, C), BF),
            pltpu.VMEM((2 * ROWS, TAP_ROWS), BF),
            pltpu.VMEM((2 * ROWS, C), F32),
            pltpu.SemaphoreType.DMA((STAGE,)),
        ],
    )(at, unit, slopes, metric, *pieces)


def to_units(lanczos_block, slope, metric, z, y, x, c):
    p = z // 2
    block = lanczos_block.reshape(K, 2, 4, 8, C)
    block = lax.dynamic_index_in_dim(block, p, 2, keepdims=False)
    head = lax.reduce_precision(metric, 8, 7)
    rest = metric - head
    middle = lax.reduce_precision(rest, 8, 7)
    low = rest - middle
    parts = jnp.stack([head, middle, low, jnp.zeros_like(low)], -1).astype(BF)
    parts = lax.dynamic_index_in_dim(parts.reshape(2, 4, 8, 4), p, 1, keepdims=False)
    parts = jnp.broadcast_to(parts[..., None], (2, 8, 4, 128)).reshape(1, 2, 8, C)
    both = jnp.concatenate([block, slope, parts])
    both = both.reshape(21, 2, 2, 4, C).transpose(3, 0, 1, 2, 4)
    both = swap(both, x, shift_x)
    block = both[:, :16].reshape(4, 2, 4, 2, 2, 2, C).transpose(2, 3, 1, 0, 4, 5, 6)
    fixed = jnp.broadcast_to(both[None, :, 16:], (4, 4, 5, 2, 2, C))
    fixed = fixed.transpose(0, 2, 1, 3, 4, 5)
    both = jnp.concatenate([block.reshape(4, 4, 4, 2, 2, C), fixed], 1)
    both = swap(both, y, shift_y)
    mine = lax.dynamic_slice_in_dim(both, c * 2, 2, 1)
    theirs = lax.dynamic_slice_in_dim(both, 2 - c * 2, 2, 1)
    fixed = both[:, 4:]
    kept = jnp.concatenate([mine, fixed], 1)
    sent = jnp.concatenate([theirs, fixed], 1)
    sent = shift_c(sent, 1)
    both = place([kept, sent], c)
    both = both.transpose(2, 4, 1, 3, 0, 5, 6).reshape(7, 2, 64, C)
    unit = both[:2].transpose(1, 0, 2, 3).reshape(2 * ROWS, C)
    return unit, both[2:6].reshape(STAGE, ROWS, C), both[6].reshape(ROWS, C)


def to_rows(unit, y, x, c):
    unit = unit.reshape(2, 2, 4, 4, 2, 2, C)
    lower = lax.ppermute(unit[0], "section", [(2 * p, p) for p in range(4)])
    upper = lax.ppermute(unit[1], "section", [(2 * p, p + 4) for p in range(4)])
    both = lower + upper
    both = swap(both.transpose(3, 0, 1, 2, 4, 5), c, shift_c)
    both = swap(both.transpose(3, 0, 1, 2, 4, 5), x, shift_x)
    both = swap(both.transpose(3, 0, 1, 2, 4, 5), y, shift_y)
    return both.transpose(3, 0, 2, 4, 1, 5).reshape(K, 8, C)


def all_sum(v):
    for bit in (1, 2, 4, 8, 16):
        v = v + lax.ppermute(v, "lon", [(i, i ^ bit) for i in range(32)])
    for bit in (1, 2, 4):
        v = v + lax.ppermute(v, "section", [(i, i ^ bit) for i in range(8)])
    return v


def body(lanczos_block, previous, beta_prev, weights, act_slope, metric):
    z = lax.axis_index("section")
    b = lax.axis_index("lon")
    y, x, c = b // 8, (b // 2) % 4, b % 2
    pieces, slopes = fetch_layers(weights[0], act_slope[0], z, y, x, c)
    unit, slopes, scale = to_units(lanczos_block, slopes, metric, z, y, x, c)
    at = jnp.stack([z, y, x, c]).astype(jnp.int32)
    rest = (slopes, scale, pieces)
    unit = run_passes(0, True, False, at, unit, *rest)
    unit = lax.ppermute(unit, "section", [(2 * p, 2 * p + 1) for p in range(4)])
    unit = run_passes(1, True, True, at, unit, *rest)
    unit = lax.ppermute(unit, "section", [(2 * p + 1, 2 * p) for p in range(4)])
    unit = run_passes(0, False, True, at, unit, *rest)
    applied = to_rows(unit, y, x, c)
    high = lax.Precision.HIGHEST
    cells = float(8 * 256 * C)
    own = lax.dynamic_slice_in_dim(lanczos_block, z, 1, 1).reshape(K, -1).astype(F32)
    before = previous.reshape(K, -1).astype(F32)
    shifted = applied.reshape(K, -1).astype(F32) - jnp.dot(beta_prev, before, precision=high)

    def inner(u, v):
        return lax.dot_general(u, v, (((1,), (1,)), ((), ())), precision=high)

    sums = jnp.concatenate([inner(own, shifted), inner(shifted, shifted), inner(own, own)])
    sums = all_sum(sums) / cells
    projection, squares, base = sums[:K], sums[K : 2 * K], sums[2 * K :]
    residual = shifted - jnp.dot(projection.T, own, precision=high)
    cross = jnp.dot(projection.T, projection, precision=high)
    twice = jnp.dot(jnp.dot(projection.T, base, precision=high), projection, precision=high)
    gram = squares - cross - cross.T + twice
    return residual.reshape(K, 1, 8, C), projection, gram


def solution(mesh):
    return jax.shard_map(
        body,
        mesh=mesh,
        in_specs=(
            P(None, None, "lon", None),
            P(None, "section", "lon", None),
            P(),
            P("section", None, None, None),
            P("section", None, "lon", None),
            P(None, "lon"),
        ),
        out_specs=(P(None, "section", "lon", None), P(), P()),
        check_vma=False,
    )
```
